32 devices in a mesh: grp: 2 (over x), ka: 16 (over z, y, core).
Axes of the slice: x: 2, y: 2, z: 4, core: 2. Of those that a mesh axis runs over, the one named last changes fastest.
Arguments:
- sources: bfloat16 [1024, 512, 64], P('ka', None, 'grp'), parts along dimension 2, may hold values from -6 to 6
- bessel: bfloat16 [512, 1024, 512], P('ka'), may hold values from -0.25 to 0.25
- multipoles: int32 [512], P('ka'), may hold values from 2 to 5000
- window_low: int32 [64], P('grp'), parts along dimension 0, may hold values from 0 to 127
- window_high: int32 [64], P('grp'), parts along dimension 0, may hold values from 384 to 512
- params: float32 [6, 64], P(None, 'grp'), parts along dimension 1, may hold values from -1 to 1
- weight_in: float32 [512, 6], replicated, may hold values from -2.5 to 2.5
- bias_in: float32 [512], replicated, may hold values from -3 to 3
- weight_mid: float32 [512, 512], replicated, may hold values from -0.25 to 0.25
- bias_mid: float32 [512], replicated, may hold values from -3 to 3
- weight_out: float32 [64, 512], replicated, may hold values from -0.25 to 0.25
- bias_out: float32 [64], replicated, may hold values from -4 to 4
- pca_basis: float32 [512, 64], P('ka'), may hold values from -0.75 to 0.75
- offset: float32 [512], P('ka'), may hold values from -4 to 4
Outputs:
- spectra: float32 [512, 64], P('ka', 'grp'), parts along dimension 1
- grad_basis: float32 [1024, 64], P(('grp', 'ka')), parts along dimension 0
- grad_weight_in: float32 [1024, 6], P('grp'), parts along dimension 0
- grad_weight_mid: float32 [1024, 512], P('grp'), parts along dimension 0
- grad_weight_out: float32 [128, 512], P('grp'), parts along dimension 0
The draws below stay inside these ranges and needn't reach their ends.
There are 2 independent parts, one for each index of `grp`. The reference program is written for one: setup_inputs(seed, part) draws one part's arguments, and reference() takes and returns one part's arrays. A program takes and returns all parts, laid end to end along the dimension named above; an argument that names none is the same for every part. Nothing has to cross between parts.
All inputs are finite; a program needn't handle non-finite values.
Results may differ from the reference program's by a relative error of at most 0.0003.
Values may be sent and summed in bfloat16 or wider, within the bound.
A program may use at most 128 MiB of HBM per device.

```python
import math
import jax
import jax.numpy as jnp
from jax import lax

NT = 1024
NK = 512
NL = 512
LMAX = 5000
NPAR = 6
HID = 512
PCA = 64
C = 32


def place_ends(array, own_key, smallest, largest):
    extent = array.shape
    index_at = [jax.random.randint(jax.random.fold_in(own_key, axis), (), 0, extent[axis]) for axis in range(len(extent))]
    array = array.at[tuple(index_at)].set(smallest)
    longest = extent.index(max(extent))
    index_at[longest] = (index_at[longest] + 1) % extent[longest]
    return array.at[tuple(index_at)].set(largest)


def raised(result, own_key, source, target, parts, factor):
    def block_of(dim):
        return (jnp.arange(result.shape[dim]) // (result.shape[dim] // parts)).reshape((-1,) + (1,) * (result.ndim - 1 - dim))

    near = jax.random.permutation(own_key, parts)[block_of(target)]
    second = (block_of(target) + parts // 2) % parts
    return jnp.where((block_of(source) == near) | (block_of(source) == second), factor * result, result)


def block_levels(stream_key, dims, pieces, smallest, top_value):
    factor_of, own = 1.0, jax.random.fold_in(stream_key, 6)
    for position, parts in pieces:
        steps = jnp.exp(jax.random.uniform(jax.random.fold_in(own, position), (parts,), jnp.float32, smallest / len(pieces), top_value / len(pieces)))
        factor_of = factor_of * jnp.repeat(steps, dims[position] // parts).reshape([-1 if axis == position else 1 for axis in range(len(dims))])
    return factor_of


def noise(own_key, shape, width, reach, cuts=(), kind=jnp.bfloat16):
    drawn = jax.random.normal(own_key, shape, jnp.float32) * width
    if len(cuts) > 0:
        drawn = block_levels(own_key, shape, cuts, -0.22, 0.18) * drawn
    return jnp.clip(drawn, min=-reach, max=reach).astype(kind)


def bell_draw_with(key, extent, scale, most, split, heavy, kind=jnp.bfloat16):
    drawn = scale * jax.random.normal(key, extent, jnp.float32)
    if split:
        drawn = drawn * block_levels(key, extent, split, -0.22, 0.18)
    return jnp.clip(raised(drawn, jax.random.fold_in(key, 3), *heavy), -most, most).astype(kind)


def setup_inputs(seed: int = 0, part: int = 0) -> dict:
    splits = jax.random.split(jax.random.key(seed), 15)
    part_splits = jax.random.split(jax.random.fold_in(splits[14], part), 15)
    sources = noise(part_splits[0], (NT, NK, C), 1.0, 6.0, ((0, 16),))
    bessel = bell_draw_with(splits[1], (NK, NT, NL), NT ** -0.5, 0.25, ((0, 16),), (0, 2, 16, 2.0))
    multipoles = place_ends(jax.random.randint(splits[2], (NL,), 2, LMAX + 1), jax.random.fold_in(splits[2], 1), 2, LMAX).astype(jnp.int32)
    window_low = place_ends(jax.random.randint(part_splits[3], (C,), 0, NK // 4), jax.random.fold_in(part_splits[3], 1), 0, (NK // 4) - 1).astype(jnp.int32)
    window_high = place_ends(jax.random.randint(part_splits[4], (C,), (3 * NK) // 4, NK + 1), jax.random.fold_in(part_splits[4], 1), (3 * NK) // 4, NK).astype(jnp.int32)
    params = jnp.clip(jax.random.uniform(part_splits[5], (NPAR, C), jnp.float32, -1.0, 1.0), -1.0, 1.0)
    weight_in = noise(splits[6], (HID, NPAR), NPAR ** -0.5, 2.5, (), jnp.float32)
    bias_in = noise(splits[7], (HID,), 0.5, 3.0, (), jnp.float32)
    weight_mid = noise(splits[8], (HID, HID), HID ** -0.5, 0.25, (), jnp.float32)
    bias_mid = noise(splits[9], (HID,), 0.5, 3.0, (), jnp.float32)
    weight_out = noise(splits[10], (PCA, HID), HID ** -0.5, 0.25, (), jnp.float32)
    bias_out = noise(splits[11], (PCA,), 1.0, 4.0, (), jnp.float32)
    pca_basis = noise(splits[12], (NL, PCA), PCA ** -0.5, 0.75, ((0, 16),), jnp.float32)
    offset = noise(splits[13], (NL,), 1.0, 4.0, ((0, 16),), jnp.float32)
    return {"sources": sources, "bessel": bessel, "multipoles": multipoles, "window_low": window_low, "window_high": window_high, "params": params, "weight_in": weight_in, "bias_in": bias_in, "weight_mid": weight_mid, "bias_mid": bias_mid, "weight_out": weight_out, "bias_out": bias_out, "pca_basis": pca_basis, "offset": offset}


def primordial(params, window_low, window_high, first_wave, wave_count, total_waves):
    wave_index = first_wave + jnp.arange(wave_count, dtype=jnp.int32)
    log_ratio = math.log(0.002) + wave_index.astype(jnp.float32) * (math.log(5000.0) / total_waves)
    tilted = 0.5 * params[0][None, :] + 0.3 * params[1][None, :] * log_ratio[:, None]
    inside = (wave_index[:, None] >= window_low[None, :]) & (wave_index[:, None] < window_high[None, :])
    return jnp.where(inside, jnp.exp(tilted), jnp.zeros_like(tilted)) / total_waves


def silu_slope(value):
    sigma = jax.nn.sigmoid(value)
    return sigma * (1.0 + value * (1.0 - sigma))


def mat(left, right):
    return jnp.dot(left, right, precision=lax.Precision.HIGHEST)


def reference(sources, bessel, multipoles, window_low, window_high, params, weight_in, bias_in, weight_mid, bias_mid, weight_out, bias_out, pca_basis, offset):
    block_size = 16
    cosmos = params.shape[1]

    def accumulate(total, block_id):
        first_wave = block_id * block_size
        source_block = lax.dynamic_slice_in_dim(sources, first_wave, block_size, 1).astype(jnp.float32)
        kernel = lax.dynamic_slice_in_dim(bessel, first_wave, block_size, 0).astype(jnp.float32)
        transfer = jnp.einsum("tkc,ktl->klc", source_block, kernel, precision=lax.Precision.HIGHEST)
        factor = primordial(params, window_low, window_high, first_wave, block_size, NK)
        return total + jnp.einsum("klc,kc->lc", transfer * transfer, factor, precision=lax.Precision.HIGHEST), None

    power, _ = lax.scan(accumulate, jnp.zeros((NL, cosmos), jnp.float32), jnp.arange(NK // block_size, dtype=jnp.int32))
    degree = multipoles.astype(jnp.float32)
    smoothing = jnp.exp(-2.0 * degree * (degree + 1.0) / (LMAX * (LMAX + 1.0)))
    spectra = smoothing[:, None] * power

    inner_pre = mat(weight_in, params) + bias_in[:, None]
    inner_act = jax.nn.silu(inner_pre)
    middle_pre = mat(weight_mid, inner_act) + bias_mid[:, None]
    middle_act = jax.nn.silu(middle_pre)
    coeffs = mat(weight_out, middle_act) + bias_out[:, None]
    residual = offset[:, None] + mat(pca_basis, coeffs) - spectra
    grad_basis = mat(residual, coeffs.T) / cosmos
    coef_grad = mat(pca_basis.T, residual) / cosmos
    grad_weight_out = mat(coef_grad, middle_act.T)
    middle_delta = mat(weight_out.T, coef_grad) * silu_slope(middle_pre)
    grad_weight_mid = mat(middle_delta, inner_act.T)
    inner_delta = mat(weight_mid.T, middle_delta) * silu_slope(inner_pre)
    grad_weight_in = mat(inner_delta, params.T)
    return (spectra, grad_basis, grad_weight_in, grad_weight_mid, grad_weight_out)
```

```python
import functools
import math

import jax
import jax.numpy as jnp
from jax import lax
from jax.experimental import pallas as pl
from jax.experimental.pallas import tpu as pltpu
from jax.sharding import PartitionSpec as P

MESH = pl.DeviceIdType.MESH
LANES = 128

LMAX = 5000


def primordial(params, window_low, window_high, first_wave, wave_count, total_waves):
    wave_index = first_wave + jnp.arange(wave_count, dtype=jnp.int32)
    log_ratio = math.log(0.002) + wave_index.astype(jnp.float32) * (math.log(5000.0) / total_waves)
    tilted = 0.5 * params[0][None, :] + 0.3 * params[1][None, :] * log_ratio[:, None]
    inside = (wave_index[:, None] >= window_low[None, :]) & (
        wave_index[:, None] < window_high[None, :]
    )
    return jnp.where(inside, jnp.exp(tilted), jnp.zeros_like(tilted)) / total_waves


def silu_slope(value):
    sigma = jax.nn.sigmoid(value)
    return sigma * (1.0 + value * (1.0 - sigma))


def mat(left, right):
    return jnp.dot(left, right, precision=lax.Precision.HIGHEST)


def backward(
    coef_grad, inner_pre, inner_act, middle_pre, middle_act, params, weight_mid, weight_out
):
    grad_out = mat(coef_grad, middle_act.T)
    middle_delta = mat(weight_out.T, coef_grad) * silu_slope(middle_pre)
    grad_mid = mat(middle_delta, inner_act.T)
    inner_delta = mat(weight_mid.T, middle_delta) * silu_slope(inner_pre)
    grad_in = mat(inner_delta, params.T)
    return (grad_in, grad_mid, grad_out)


def exchange_kernel(
    n,
    cosmos,
    part_ref,
    base_ref,
    smooth_ref,
    basis_ref,
    spectra_ref,
    residual_ref,
    coef_ref,
    power_in,
    coef_out,
    coef_in,
    send_power,
    recv_power,
    send_coef,
    recv_coef,
):
    me = lax.axis_index("ka")
    barrier = pltpu.get_barrier_semaphore()
    for step in range(1, n):
        peer = lax.rem(me + step, n)
        pl.semaphore_signal(barrier, inc=1, device_id={"ka": peer}, device_id_type=MESH)
    pl.semaphore_wait(barrier, n - 1)

    def scatter(source_of, landing, send_sem, recv_sem):
        copies = []
        for step in range(1, n):
            peer = lax.rem(me + step, n)
            copy = pltpu.make_async_remote_copy(
                src_ref=source_of(peer),
                dst_ref=landing.at[me],
                send_sem=send_sem.at[step],
                recv_sem=recv_sem.at[step],
                device_id={"ka": peer},
                device_id_type=MESH,
            )
            copy.start()
            copies.append(copy)
        return copies

    copies = scatter(lambda peer: part_ref.at[peer], power_in, send_power, recv_power)
    power_in[me] = part_ref[me]
    for copy in copies:
        copy.wait()
    spectra = smooth_ref[...] * jnp.sum(power_in[...], axis=0)
    spectra_ref[...] = spectra
    residual = base_ref[...] - spectra
    residual_ref[...] = residual

    coef_out[...] = packed_coef(basis_ref, residual, cosmos)
    copies = scatter(lambda peer: coef_out, coef_in, send_coef, recv_coef)
    coef_in[me] = coef_out[...]
    for copy in copies:
        copy.wait()
    coef_ref[...] = jnp.sum(coef_in[...], axis=0)


def packed_coef(basis_ref, residual, cosmos):
    groups, components, _ = basis_ref.shape
    lane_group = lax.broadcasted_iota(jnp.int32, (components, LANES), 1) // cosmos
    spread = jnp.zeros((components, LANES), jnp.float32)
    for g in range(groups):
        spread = jnp.where(lane_group == g, mat(basis_ref[g], residual), spread)
    total = spread
    for g in range(1, groups):
        total = total + pltpu.roll(spread, g * cosmos, 1)
    rows = components // groups
    packed = total[:rows]
    for g in range(1, groups):
        packed = jnp.where(lane_group[:rows] == g, total[g * rows : (g + 1) * rows], packed)
    return packed / cosmos


def exchange(n, part, base, smooth, basis, cosmos):
    groups = LANES // cosmos
    multipoles, components = basis.shape
    rows = multipoles // groups
    block = (rows, LANES)
    coef_block = (components // groups, LANES)
    spectra, residual, coef = pl.pallas_call(
        functools.partial(exchange_kernel, n, cosmos),
        out_shape=(
            jax.ShapeDtypeStruct(block, jnp.float32),
            jax.ShapeDtypeStruct(block, jnp.float32),
            jax.ShapeDtypeStruct(coef_block, jnp.float32),
        ),
        in_specs=[pl.BlockSpec(memory_space=pltpu.VMEM)] * 4,
        out_specs=[pl.BlockSpec(memory_space=pltpu.VMEM)] * 3,
        scratch_shapes=[
            pltpu.VMEM((n,) + block, jnp.float32),
            pltpu.VMEM(coef_block, jnp.float32),
            pltpu.VMEM((n,) + coef_block, jnp.float32),
        ]
        + [pltpu.SemaphoreType.DMA((n,))] * 4,
        compiler_params=pltpu.CompilerParams(collective_id=0, has_side_effects=True),
    )(
        part.reshape((n,) + block),
        base.reshape(block),
        jnp.broadcast_to(smooth[:, None], (multipoles, cosmos)).reshape(block),
        basis.reshape(rows, groups, components).transpose(1, 2, 0),
    )
    coef = coef.reshape(components // groups, groups, cosmos).transpose(1, 0, 2).reshape(components, cosmos)
    return spectra.reshape(multipoles, cosmos), residual.reshape(multipoles, cosmos), coef


def local(
    n,
    sources,
    bessel,
    multipoles,
    window_low,
    window_high,
    params,
    weight_in,
    bias_in,
    weight_mid,
    bias_mid,
    weight_out,
    bias_out,
    pca_basis,
    offset,
):
    local_waves = bessel.shape[0]
    total_waves = sources.shape[1]
    cosmos = params.shape[1]
    first_wave = lax.axis_index("ka") * local_waves
    factor = primordial(params, window_low, window_high, first_wave, local_waves, total_waves)
    regrouped = lax.all_to_all(sources, "ka", split_axis=1, concat_axis=0, tiled=True)
    transfer = jnp.einsum("tkc,ktl->klc", regrouped, bessel, preferred_element_type=jnp.float32)
    part = jnp.einsum("klc,kc->lc", transfer * transfer, factor, precision=lax.Precision.HIGHEST)
    degree = multipoles.astype(jnp.float32)
    smoothing = jnp.exp(-2.0 * degree * (degree + 1.0) / (LMAX * (LMAX + 1.0)))
    inner_pre = mat(weight_in, params) + bias_in[:, None]
    inner_act = jax.nn.silu(inner_pre)
    middle_pre = mat(weight_mid, inner_act) + bias_mid[:, None]
    middle_act = jax.nn.silu(middle_pre)
    coeffs = mat(weight_out, middle_act) + bias_out[:, None]
    base = offset[:, None] + mat(pca_basis, coeffs)
    if packs(n, cosmos, pca_basis):
        spectra, residual, coef_grad = exchange(n, part, base, smoothing, pca_basis, cosmos)
    else:
        power = lax.psum_scatter(part, "ka", scatter_dimension=0, tiled=True)
        spectra = smoothing[:, None] * power
        residual = base - spectra
        coef_grad = lax.psum(mat(pca_basis.T, residual) / cosmos, "ka")
    grad_basis = mat(residual, coeffs.T) / cosmos
    grad_in, grad_mid, grad_out = backward(
        coef_grad, inner_pre, inner_act, middle_pre, middle_act, params, weight_mid, weight_out
    )
    return (spectra, grad_basis, grad_in, grad_mid, grad_out)


def packs(n, cosmos, basis):
    if n > 32 or LANES % cosmos:
        return False
    groups = LANES // cosmos
    return basis.shape[0] % (8 * groups) == 0 and basis.shape[1] % (8 * groups) == 0


def solution(mesh):
    return jax.shard_map(
        functools.partial(local, mesh.shape["ka"]),
        mesh=mesh,
        in_specs=(
            P("ka", None, "grp"),
            P("ka", None, None),
            P("ka"),
            P("grp"),
            P("grp"),
            P(None, "grp"),
            P(),
            P(),
            P(),
            P(),
            P(),
            P(),
            P("ka", None),
            P("ka"),
        ),
        out_specs=(
            P("ka", "grp"),
            P(("grp", "ka"), None),
            P("grp", None),
            P("grp", None),
            P("grp", None),
        ),
        check_vma=False,
    )
```

```python
import functools
import math

import jax
import jax.numpy as jnp
from jax import lax
from jax.experimental import pallas as pl
from jax.experimental.pallas import tpu as pltpu
from jax.sharding import PartitionSpec as P

MESH = pl.DeviceIdType.MESH
LANES = 128
FAN = 4

LMAX = 5000


def primordial(params, window_low, window_high, first_wave, wave_count, total_waves):
    wave_index = first_wave + jnp.arange(wave_count, dtype=jnp.int32)
    log_ratio = math.log(0.002) + wave_index.astype(jnp.float32) * (math.log(5000.0) / total_waves)
    tilted = 0.5 * params[0][None, :] + 0.3 * params[1][None, :] * log_ratio[:, None]
    inside = (wave_index[:, None] >= window_low[None, :]) & (
        wave_index[:, None] < window_high[None, :]
    )
    return jnp.where(inside, jnp.exp(tilted), jnp.zeros_like(tilted)) / total_waves


def silu_slope(value):
    sigma = jax.nn.sigmoid(value)
    return sigma * (1.0 + value * (1.0 - sigma))


def mat(left, right):
    return jnp.dot(left, right, precision=lax.Precision.HIGHEST)


def backward(
    coef_grad, inner_pre, inner_act, middle_pre, middle_act, params, weight_mid, weight_out
):
    grad_out = mat(coef_grad, middle_act.T)
    middle_delta = mat(weight_out.T, coef_grad) * silu_slope(middle_pre)
    grad_mid = mat(middle_delta, inner_act.T)
    inner_delta = mat(weight_mid.T, middle_delta) * silu_slope(inner_pre)
    grad_in = mat(inner_delta, params.T)
    return (grad_in, grad_mid, grad_out)


def exchange_kernel(
    n,
    cosmos,
    part_ref,
    base_ref,
    smooth_ref,
    basis_ref,
    spectra_ref,
    residual_ref,
    coef_ref,
    power_in,
    coef_out,
    coef_in,
    send_power,
    recv_power,
    send_coef,
    recv_coef,
):
    me = lax.axis_index("ka")
    barrier = pltpu.get_barrier_semaphore()
    for step in range(1, n):
        peer = lax.rem(me + step, n)
        pl.semaphore_signal(barrier, inc=1, device_id={"ka": peer}, device_id_type=MESH)
    pl.semaphore_wait(barrier, n - 1)

    def scatter(source_of, landing, send_sem, recv_sem):
        copies = []
        for step in range(1, n):
            peer = lax.rem(me + step, n)
            copy = pltpu.make_async_remote_copy(
                src_ref=source_of(peer),
                dst_ref=landing.at[me],
                send_sem=send_sem.at[step],
                recv_sem=recv_sem.at[step],
                device_id={"ka": peer},
                device_id_type=MESH,
            )
            copy.start()
            copies.append(copy)
        return copies

    copies = scatter(lambda peer: part_ref.at[peer], power_in, send_power, recv_power)
    power_in[me] = part_ref[me]
    for copy in copies:
        copy.wait()
    spectra = smooth_ref[...] * jnp.sum(power_in[...], axis=0)
    spectra_ref[...] = spectra
    residual = base_ref[...] - spectra
    residual_ref[...] = residual

    coef_out[...] = packed_coef(basis_ref, residual, cosmos)
    copies = scatter(lambda peer: coef_out, coef_in, send_coef, recv_coef)
    coef_in[me] = coef_out[...]
    for copy in copies:
        copy.wait()
    coef_ref[...] = jnp.sum(coef_in[...], axis=0)


def packed_coef(basis_ref, residual, cosmos):
    groups, components, _ = basis_ref.shape
    lane_group = lax.broadcasted_iota(jnp.int32, (components, LANES), 1) // cosmos
    spread = jnp.zeros((components, LANES), jnp.float32)
    for g in range(groups):
        spread = jnp.where(lane_group == g, mat(basis_ref[g], residual), spread)
    total = spread
    for g in range(1, groups):
        total = total + pltpu.roll(spread, g * cosmos, 1)
    rows = components // groups
    packed = total[:rows]
    for g in range(1, groups):
        packed = jnp.where(lane_group[:rows] == g, total[g * rows : (g + 1) * rows], packed)
    return packed / cosmos


def exchange(n, part, base, smooth, basis, cosmos):
    groups = LANES // cosmos
    multipoles, components = basis.shape
    rows = multipoles // groups
    block = (rows, LANES)
    coef_block = (components // groups, LANES)
    spectra, residual, coef = pl.pallas_call(
        functools.partial(exchange_kernel, n, cosmos),
        out_shape=(
            jax.ShapeDtypeStruct(block, jnp.float32),
            jax.ShapeDtypeStruct(block, jnp.float32),
            jax.ShapeDtypeStruct(coef_block, jnp.float32),
        ),
        in_specs=[pl.BlockSpec(memory_space=pltpu.VMEM)] * 4,
        out_specs=[pl.BlockSpec(memory_space=pltpu.VMEM)] * 3,
        scratch_shapes=[
            pltpu.VMEM((n,) + block, jnp.float32),
            pltpu.VMEM(coef_block, jnp.float32),
            pltpu.VMEM((n,) + coef_block, jnp.float32),
        ]
        + [pltpu.SemaphoreType.DMA((n,))] * 4,
        compiler_params=pltpu.CompilerParams(collective_id=0, has_side_effects=True),
    )(
        part.reshape((n,) + block),
        base.reshape(block),
        jnp.broadcast_to(smooth[:, None], (multipoles, cosmos)).reshape(block),
        basis.reshape(rows, groups, components).transpose(1, 2, 0),
    )
    coef = coef.reshape(components // groups, groups, cosmos).transpose(1, 0, 2).reshape(components, cosmos)
    return spectra.reshape(multipoles, cosmos), residual.reshape(multipoles, cosmos), coef


def flipped(level, bits, levels):
    result, weight = 0, 1
    while weight < levels:
        bit = lax.rem(level // weight, 2)
        result = result + weight * (1 - bit if bits // weight % 2 else bit)
        weight *= 2
    return result


def transfer_kernel(
    n,
    source_ref,
    bessel_ref,
    factor_ref,
    part_ref,
    wide,
    turned,
    packed,
    landed,
    kernels,
    total,
    send_sem,
    recv_sem,
    load_sem,
):
    times, cosmos, _ = source_ref.shape
    waves = factor_ref.shape[0]
    half = cosmos // 2
    levels = n // FAN
    me = lax.axis_index("ka")
    my_level, my_place = me // FAN, lax.rem(me, FAN)

    barrier = pltpu.get_barrier_semaphore()
    for step in range(1, n):
        peer = lax.rem(me + step, n)
        pl.semaphore_signal(barrier, inc=1, device_id={"ka": peer}, device_id_type=MESH)

    loads = []
    for i in range(levels):
        span = pl.ds(pl.multiple_of(flipped(my_level, i, levels) * (FAN * times), FAN * times), FAN * times)
        load = pltpu.make_async_copy(bessel_ref.at[:, span, :], kernels.at[i], load_sem.at[i])
        load.start()
        loads.append(load)

    copies = {}
    far_first = sorted(range(1, levels), key=lambda i: (-(i // (levels // 2)), i)) + [0]
    for position, i in enumerate(far_first):
        level = flipped(my_level, i, levels)
        lanes = pl.ds(pl.multiple_of(level * LANES, LANES), LANES)
        wide[...] = source_ref[:, :, lanes].astype(jnp.float32).reshape(times * cosmos, LANES)
        for c in range(half):
            pair = jnp.concatenate(
                [wide[pl.ds(c, times, stride=cosmos), :], wide[pl.ds(c + half, times, stride=cosmos), :]], axis=0
            )
            turned[pl.ds(c, LANES, stride=half), :] = pair.T
        packed[pl.ds(level * FAN, FAN)] = turned[...].astype(jnp.bfloat16).reshape(FAN, waves * half, LANES)
        if position == 0:
            pl.semaphore_wait(barrier, n - 1)
        for step in range(FAN):
            if i == 0 and step == 0:
                continue
            peer = level * FAN + lax.rem(my_place + step, FAN)
            copy = pltpu.make_async_remote_copy(
                src_ref=packed.at[peer],
                dst_ref=landed.at[me],
                send_sem=send_sem.at[i * FAN + step],
                recv_sem=recv_sem.at[i * FAN + step],
                device_id={"ka": peer},
                device_id_type=MESH,
            )
            copy.start()
            copies[i, step] = copy
    landed[me] = packed[me]
    part_ref[...] = jnp.zeros_like(part_ref)

    low_lanes = lax.broadcasted_iota(jnp.int32, (half, LANES), 1) < times

    def joined(first, second):
        first, second = first.astype(jnp.float32), second.astype(jnp.float32)
        low = jnp.where(low_lanes, first, pltpu.roll(second, times, 1))
        high = jnp.where(low_lanes, pltpu.roll(first, times, 1), second)
        return jnp.concatenate([low, high], axis=0).astype(jnp.bfloat16)

    for i in range(levels):
        level = flipped(my_level, i, levels)
        for step in range(FAN):
            if (i, step) in copies:
                copies[i, step].wait_recv()
        loads[i].wait()

        def wave(k, carry, i=i, level=level):
            rows = pl.ds(pl.multiple_of(k * half, half), half)
            blocks = [landed[level * FAN + place, rows, :] for place in range(FAN)]
            left = jnp.concatenate([joined(*blocks[p : p + 2]) for p in range(0, FAN, 2)], axis=1)
            product = jnp.dot(left, kernels[i, k], preferred_element_type=jnp.float32)
            if i > 0:
                product = product + total[k]
            if i < levels - 1:
                total[k] = product
            else:
                part_ref[...] += factor_ref[k] * product * product
            return carry

        lax.fori_loop(0, waves, wave, 0, unroll=4)
    for copy in copies.values():
        copy.wait_send()


def landed_power(n, sources, bessel, factor):
    times, _, cosmos = sources.shape
    waves, _, multipoles = bessel.shape
    levels = n // FAN
    block = (n, waves * cosmos // 2, LANES)
    return pl.pallas_call(
        functools.partial(transfer_kernel, n),
        out_shape=jax.ShapeDtypeStruct((cosmos, multipoles), jnp.float32),
        in_specs=[
            pl.BlockSpec(memory_space=pltpu.VMEM),
            pl.BlockSpec(memory_space=pl.ANY),
            pl.BlockSpec(memory_space=pltpu.VMEM),
        ],
        out_specs=pl.BlockSpec(memory_space=pltpu.VMEM),
        scratch_shapes=[
            pltpu.VMEM((times * cosmos, LANES), jnp.float32),
            pltpu.VMEM((LANES * cosmos // 2, LANES), jnp.float32),
            pltpu.VMEM(block, jnp.bfloat16),
            pltpu.VMEM(block, jnp.bfloat16),
            pltpu.VMEM((levels, waves, FAN * times, multipoles), jnp.bfloat16),
            pltpu.VMEM((waves, cosmos, multipoles), jnp.float32),
            pltpu.SemaphoreType.DMA((n,)),
            pltpu.SemaphoreType.DMA((n,)),
            pltpu.SemaphoreType.DMA((levels,)),
        ],
        compiler_params=pltpu.CompilerParams(
            collective_id=1, has_side_effects=True, vmem_limit_bytes=52 * 1024 * 1024
        ),
        cost_estimate=pl.CostEstimate(
            flops=2 * bessel.size * cosmos, bytes_accessed=2 * (bessel.size + sources.size), transcendentals=0
        ),
    )(sources.transpose(0, 2, 1), bessel, factor[:, :, None]).T


def local(
    n,
    sources,
    bessel,
    multipoles,
    window_low,
    window_high,
    params,
    weight_in,
    bias_in,
    weight_mid,
    bias_mid,
    weight_out,
    bias_out,
    pca_basis,
    offset,
):
    local_waves = bessel.shape[0]
    total_waves = sources.shape[1]
    cosmos = params.shape[1]
    first_wave = lax.axis_index("ka") * local_waves
    factor = primordial(params, window_low, window_high, first_wave, local_waves, total_waves)
    if lands(n, sources, bessel):
        part = landed_power(n, sources, bessel, factor)
    else:
        regrouped = lax.all_to_all(sources, "ka", split_axis=1, concat_axis=0, tiled=True)
        transfer = jnp.einsum("tkc,ktl->klc", regrouped, bessel, preferred_element_type=jnp.float32)
        part = jnp.einsum("klc,kc->lc", transfer * transfer, factor, precision=lax.Precision.HIGHEST)
    degree = multipoles.astype(jnp.float32)
    smoothing = jnp.exp(-2.0 * degree * (degree + 1.0) / (LMAX * (LMAX + 1.0)))
    inner_pre = mat(weight_in, params) + bias_in[:, None]
    inner_act = jax.nn.silu(inner_pre)
    middle_pre = mat(weight_mid, inner_act) + bias_mid[:, None]
    middle_act = jax.nn.silu(middle_pre)
    coeffs = mat(weight_out, middle_act) + bias_out[:, None]
    base = offset[:, None] + mat(pca_basis, coeffs)
    if packs(n, cosmos, pca_basis):
        spectra, residual, coef_grad = exchange(n, part, base, smoothing, pca_basis, cosmos)
    else:
        power = lax.psum_scatter(part, "ka", scatter_dimension=0, tiled=True)
        spectra = smoothing[:, None] * power
        residual = base - spectra
        coef_grad = lax.psum(mat(pca_basis.T, residual) / cosmos, "ka")
    grad_basis = mat(residual, coeffs.T) / cosmos
    grad_in, grad_mid, grad_out = backward(
        coef_grad, inner_pre, inner_act, middle_pre, middle_act, params, weight_mid, weight_out
    )
    return (spectra, grad_basis, grad_in, grad_mid, grad_out)


def packs(n, cosmos, basis):
    if n > 32 or LANES % cosmos:
        return False
    groups = LANES // cosmos
    return basis.shape[0] % (8 * groups) == 0 and basis.shape[1] % (8 * groups) == 0


def lands(n, sources, bessel):
    times, _, cosmos = sources.shape
    levels = n // FAN
    return (
        2 * times == LANES
        and FAN * bessel.shape[0] == LANES
        and cosmos == 32
        and n % FAN == 0
        and levels in (2, 4)
        and bessel.shape[2] % LANES == 0
        and bessel.size * 2 <= 32 * 1024 * 1024
    )


def solution(mesh):
    return jax.shard_map(
        functools.partial(local, mesh.shape["ka"]),
        mesh=mesh,
        in_specs=(
            P("ka", None, "grp"),
            P("ka", None, None),
            P("ka"),
            P("grp"),
            P("grp"),
            P(None, "grp"),
            P(),
            P(),
            P(),
            P(),
            P(),
            P(),
            P("ka", None),
            P("ka"),
        ),
        out_specs=(
            P("ka", "grp"),
            P(("grp", "ka"), None),
            P("grp", None),
            P("grp", None),
            P("grp", None),
        ),
        check_vma=False,
    )
```

```python
import functools
import math

import jax
import jax.numpy as jnp
from jax import lax
from jax.experimental import pallas as pl
from jax.experimental.pallas import tpu as pltpu
from jax.sharding import PartitionSpec as P

MESH = pl.DeviceIdType.MESH
LANES = 128
FAN = 4

LMAX = 5000


def primordial(params, window_low, window_high, first_wave, wave_count, total_waves):
    wave_index = first_wave + jnp.arange(wave_count, dtype=jnp.int32)
    log_ratio = math.log(0.002) + wave_index.astype(jnp.float32) * (math.log(5000.0) / total_waves)
    tilted = 0.5 * params[0][None, :] + 0.3 * params[1][None, :] * log_ratio[:, None]
    inside = (wave_index[:, None] >= window_low[None, :]) & (
        wave_index[:, None] < window_high[None, :]
    )
    return jnp.where(inside, jnp.exp(tilted), jnp.zeros_like(tilted)) / total_waves


def silu_slope(value):
    sigma = jax.nn.sigmoid(value)
    return sigma * (1.0 + value * (1.0 - sigma))


def mat(left, right):
    return jnp.dot(left, right, precision=lax.Precision.HIGHEST)


def backward(
    coef_grad, inner_pre, inner_act, middle_pre, middle_act, params, weight_mid, weight_out
):
    grad_out = mat(coef_grad, middle_act.T)
    middle_delta = mat(weight_out.T, coef_grad) * silu_slope(middle_pre)
    grad_mid = mat(middle_delta, inner_act.T)
    inner_delta = mat(weight_mid.T, middle_delta) * silu_slope(inner_pre)
    grad_in = mat(inner_delta, params.T)
    return (grad_in, grad_mid, grad_out)


def contract(left, right, left_dim, right_dim):
    return lax.dot_general(
        left,
        right,
        (((left_dim,), (right_dim,)), ((), ())),
        precision=lax.Precision.HIGHEST,
        preferred_element_type=jnp.float32,
    )


def by_group(rows_of, groups, rows):
    lane_group = lax.broadcasted_iota(jnp.int32, (rows, LANES), 1) // (LANES // groups)
    packed = rows_of(0)
    for g in range(1, groups):
        packed = jnp.where(lane_group == g, rows_of(g), packed)
    return packed


def unpacked(packed, groups):
    lane_group = lax.broadcasted_iota(jnp.int32, packed.shape, 1) // (LANES // groups)
    return jnp.concatenate([jnp.where(lane_group == g, packed, 0.0) for g in range(groups)], axis=0)


def flipped(level, bits, levels):
    result, weight = 0, 1
    while weight < levels:
        bit = lax.rem(level // weight, 2)
        result = result + weight * (1 - bit if bits // weight % 2 else bit)
        weight *= 2
    return result


def transfer_kernel(
    n,
    source_ref,
    bessel_ref,
    multipoles_ref,
    low_ref,
    high_ref,
    params_ref,
    weight_in_ref,
    bias_in_ref,
    weight_mid_ref,
    bias_mid_ref,
    weight_out_ref,
    bias_out_ref,
    basis_ref,
    offset_ref,
    inner_ref,
    middle_ref,
    coeffs_ref,
    spectra_ref,
    residual_ref,
    coef_ref,
    part_ref,
    power_out,
    power_in,
    coef_out,
    coef_in,
    send_power,
    recv_power,
    send_coef,
    recv_coef,
    wide,
    turned,
    packed,
    landed,
    kernels,
    total,
    send_sem,
    recv_sem,
    load_sem,
):
    times, cosmos, _ = source_ref.shape
    waves = bessel_ref.shape[0]
    half = cosmos // 2
    levels = n // FAN
    me = lax.axis_index("ka")
    my_level, my_place = me // FAN, lax.rem(me, FAN)

    barrier = pltpu.get_barrier_semaphore()
    for step in range(1, n):
        peer = lax.rem(me + step, n)
        pl.semaphore_signal(barrier, inc=1, device_id={"ka": peer}, device_id_type=MESH)

    loads = []
    for i in range(levels):
        span = pl.ds(pl.multiple_of(flipped(my_level, i, levels) * (FAN * times), FAN * times), FAN * times)
        load = pltpu.make_async_copy(bessel_ref.at[:, span, :], kernels.at[i], load_sem.at[i])
        load.start()
        loads.append(load)

    copies = {}
    far_first = sorted(range(1, levels), key=lambda i: (-(i // (levels // 2)), i)) + [0]
    for position, i in enumerate(far_first):
        level = flipped(my_level, i, levels)
        lanes = pl.ds(pl.multiple_of(level * LANES, LANES), LANES)
        wide[...] = source_ref[:, :, lanes].astype(jnp.float32).reshape(times * cosmos, LANES)
        for c in range(half):
            pair = jnp.concatenate(
                [wide[pl.ds(c, times, stride=cosmos), :], wide[pl.ds(c + half, times, stride=cosmos), :]], axis=0
            )
            turned[pl.ds(c, LANES, stride=half), :] = pair.T
        packed[pl.ds(level * FAN, FAN)] = turned[...].astype(jnp.bfloat16).reshape(FAN, waves * half, LANES)
        if position == 0:
            pl.semaphore_wait(barrier, n - 1)
        for step in range(FAN):
            if i == 0 and step == 0:
                continue
            peer = level * FAN + lax.rem(my_place + step, FAN)
            copy = pltpu.make_async_remote_copy(
                src_ref=packed.at[peer],
                dst_ref=landed.at[me],
                send_sem=send_sem.at[i * FAN + step],
                recv_sem=recv_sem.at[i * FAN + step],
                device_id={"ka": peer},
                device_id_type=MESH,
            )
            copy.start()
            copies[i, step] = copy
    landed[me] = packed[me]
    part_ref[...] = jnp.zeros_like(part_ref)

    params = params_ref[...]
    groups, rows = LANES // basis_ref.shape[0], cosmos * basis_ref.shape[0] // LANES
    inner = contract(params, weight_in_ref[...], 0, 0) + bias_in_ref[...]
    inner_ref[...] = inner
    middle = contract(jax.nn.silu(inner), weight_mid_ref[...], 1, 1) + bias_mid_ref[...]
    middle_ref[...] = middle
    coeffs = contract(jax.nn.silu(middle), weight_out_ref[...], 1, 1) + bias_out_ref[...]
    coeffs_ref[...] = coeffs
    basis = jnp.concatenate([basis_ref[...]] * groups, axis=0)
    own = basis_ref.shape[0]
    spread = (
        lax.broadcasted_iota(jnp.int32, (own, LANES), 0) == lax.broadcasted_iota(jnp.int32, (own, LANES), 1) % own
    ).astype(jnp.float32)
    base = contract(coeffs, basis, 1, 1) + contract(offset_ref[...], spread, 1, 0)
    base = by_group(lambda g: base[g * rows : (g + 1) * rows], groups, rows)
    degree = contract(multipoles_ref[...].astype(jnp.float32), spread, 1, 0)
    smoothing = jnp.exp(-2.0 * degree * (degree + 1.0) / (LMAX * (LMAX + 1.0)))

    def column(row):
        return contract(row, jnp.ones((1, LANES), jnp.float32), 0, 0)

    amplitude, tilt = column(params_ref[0:1, :]), column(params_ref[1:2, :])
    low, high = column(low_ref[...].astype(jnp.float32)), column(high_ref[...].astype(jnp.float32))
    total_waves = source_ref.shape[2]

    def factor(k):
        index = (me * waves + k).astype(jnp.float32)
        log_ratio = math.log(0.002) + index * (math.log(5000.0) / total_waves)
        tilted = 0.5 * amplitude + 0.3 * tilt * log_ratio
        inside = (index >= low) & (index < high)
        value = jnp.where(inside, jnp.exp(tilted), 0.0) / total_waves
        return jnp.concatenate([value] * (part_ref.shape[1] // LANES), axis=1)

    low_lanes = lax.broadcasted_iota(jnp.int32, (half, LANES), 1) < times

    def joined(first, second):
        first, second = first.astype(jnp.float32), second.astype(jnp.float32)
        low = jnp.where(low_lanes, first, pltpu.roll(second, times, 1))
        high = jnp.where(low_lanes, pltpu.roll(first, times, 1), second)
        return jnp.concatenate([low, high], axis=0).astype(jnp.bfloat16)

    for i in range(levels):
        level = flipped(my_level, i, levels)
        for step in range(FAN):
            if (i, step) in copies:
                copies[i, step].wait_recv()
        loads[i].wait()

        def wave(k, carry, i=i, level=level):
            rows = pl.ds(pl.multiple_of(k * half, half), half)
            blocks = [landed[level * FAN + place, rows, :] for place in range(FAN)]
            left = jnp.concatenate([joined(*blocks[p : p + 2]) for p in range(0, FAN, 2)], axis=1)
            product = jnp.dot(left, kernels[i, k], preferred_element_type=jnp.float32)
            if i > 0:
                product = product + total[k]
            if i < levels - 1:
                total[k] = product
            else:
                part_ref[...] += factor(k) * product * product
            return carry

        lax.fori_loop(0, waves, wave, 0, unroll=4)
    for copy in copies.values():
        copy.wait_send()

    def scatter(source_of, landing, send, recv):
        started = []
        for step in range(1, n):
            peer = lax.rem(me + step, n)
            copy = pltpu.make_async_remote_copy(
                src_ref=source_of(peer),
                dst_ref=landing.at[me],
                send_sem=send.at[step],
                recv_sem=recv.at[step],
                device_id={"ka": peer},
                device_id_type=MESH,
            )
            copy.start()
            started.append(copy)
        return started

    for peer in range(n):
        lane, shift = peer * own // LANES * LANES, peer * own % LANES
        power_out[peer] = by_group(
            lambda g: pltpu.roll(
                part_ref[g * rows : (g + 1) * rows, lane : lane + LANES], (g * own - shift) % LANES, 1
            ),
            groups,
            rows,
        )
    started = scatter(lambda peer: power_out.at[peer], power_in, send_power, recv_power)
    power_in[me] = power_out[me]
    for copy in started:
        copy.wait()
    spectra = smoothing * jnp.sum(power_in[...], axis=0)
    spectra_ref[...] = spectra
    residual = base - spectra
    residual_ref[...] = residual
    gradient = contract(unpacked(residual, groups), jnp.concatenate([basis, basis], axis=1), 1, 0) / cosmos
    coef_out[...] = by_group(lambda g: gradient[g * half : (g + 1) * half], 2, half)
    started = scatter(lambda peer: coef_out, coef_in, send_coef, recv_coef)
    coef_in[me] = coef_out[...]
    for copy in started:
        copy.wait()
    coef_ref[...] = jnp.sum(coef_in[...], axis=0)


def output_kernel(
    inner_ref,
    middle_ref,
    coeffs_ref,
    packed_spectra_ref,
    residual_ref,
    coef_ref,
    params_ref,
    weight_mid_ref,
    weight_out_ref,
    spectra_ref,
    grad_basis_ref,
    grad_in_ref,
    grad_mid_ref,
    grad_out_ref,
):
    own, components = grad_basis_ref.shape
    groups = LANES // own
    cosmos = params_ref.shape[1]

    def folded(rows):
        total = rows[:own]
        for g in range(1, groups):
            total = total + rows[g * own : (g + 1) * own]
        return total

    spectra_ref[...] = folded(unpacked(packed_spectra_ref[...], groups).T)
    grad_basis_ref[...] = folded(contract(unpacked(residual_ref[...], groups), coeffs_ref[...], 0, 0)) / cosmos
    coef = coef_ref[...]
    coef = jnp.concatenate([coef, pltpu.roll(coef, components, 1)], axis=0)[:, :components]
    inner, middle = inner_ref[...], middle_ref[...]
    grad_out_ref[...] = contract(coef, jax.nn.silu(middle), 0, 0)
    middle_delta = contract(coef, weight_out_ref[...], 1, 0) * silu_slope(middle)
    grad_mid_ref[...] = contract(middle_delta, jax.nn.silu(inner), 0, 0)
    inner_delta = contract(middle_delta, weight_mid_ref[...], 1, 0) * silu_slope(inner)
    grad_in_ref[...] = contract(params_ref[...], inner_delta, 1, 0)


def landed(
    n,
    sources,
    bessel,
    multipoles,
    window_low,
    window_high,
    params,
    weight_in,
    bias_in,
    weight_mid,
    bias_mid,
    weight_out,
    bias_out,
    pca_basis,
    offset,
):
    times, _, cosmos = sources.shape
    waves, _, all_multipoles = bessel.shape
    hidden, (own, components) = weight_mid.shape[0], pca_basis.shape
    levels = n // FAN
    block = (n, waves * cosmos // 2, LANES)
    power_block, coef_block = (cosmos * own // LANES, LANES), (cosmos // 2, LANES)
    vmem = pl.BlockSpec(memory_space=pltpu.VMEM)
    results = pl.pallas_call(
        functools.partial(transfer_kernel, n),
        out_shape=[
            jax.ShapeDtypeStruct(shape, jnp.float32)
            for shape in (
                (cosmos, hidden),
                (cosmos, hidden),
                (cosmos, components),
                power_block,
                power_block,
                coef_block,
            )
        ],
        in_specs=[vmem, pl.BlockSpec(memory_space=pl.ANY)] + [vmem] * 12,
        out_specs=[vmem] * 6,
        scratch_shapes=[
            pltpu.VMEM((cosmos, all_multipoles), jnp.float32),
            pltpu.VMEM((n,) + power_block, jnp.float32),
            pltpu.VMEM((n,) + power_block, jnp.float32),
            pltpu.VMEM(coef_block, jnp.float32),
            pltpu.VMEM((n,) + coef_block, jnp.float32),
        ]
        + [pltpu.SemaphoreType.DMA((n,))] * 4
        + [
            pltpu.VMEM((times * cosmos, LANES), jnp.float32),
            pltpu.VMEM((LANES * cosmos // 2, LANES), jnp.float32),
            pltpu.VMEM(block, jnp.bfloat16),
            pltpu.VMEM(block, jnp.bfloat16),
            pltpu.VMEM((levels, waves, FAN * times, all_multipoles), jnp.bfloat16),
            pltpu.VMEM((waves, cosmos, all_multipoles), jnp.float32),
            pltpu.SemaphoreType.DMA((n,)),
            pltpu.SemaphoreType.DMA((n,)),
            pltpu.SemaphoreType.DMA((levels,)),
        ],
        compiler_params=pltpu.CompilerParams(
            collective_id=0, has_side_effects=True, vmem_limit_bytes=52 * 1024 * 1024
        ),
    )(
        sources.transpose(0, 2, 1),
        bessel,
        multipoles[None, :],
        window_low[None, :],
        window_high[None, :],
        params,
        weight_in.T,
        bias_in[None, :],
        weight_mid,
        bias_mid[None, :],
        weight_out,
        bias_out[None, :],
        pca_basis,
        offset[None, :],
    )
    spectra, grad_basis, grad_in, grad_mid, grad_out = pl.pallas_call(
        output_kernel,
        out_shape=[
            jax.ShapeDtypeStruct(shape, jnp.float32)
            for shape in (
                (own, cosmos),
                (own, components),
                (params.shape[0], hidden),
                (hidden, hidden),
                (components, hidden),
            )
        ],
        in_specs=[vmem] * 9,
        out_specs=[vmem] * 5,
    )(*results, params, weight_mid, weight_out)
    return (spectra, grad_basis, grad_in.T, grad_mid, grad_out)


def local(
    n,
    sources,
    bessel,
    multipoles,
    window_low,
    window_high,
    params,
    weight_in,
    bias_in,
    weight_mid,
    bias_mid,
    weight_out,
    bias_out,
    pca_basis,
    offset,
):
    if lands(n, sources, bessel, pca_basis):
        return landed(
            n,
            sources,
            bessel,
            multipoles,
            window_low,
            window_high,
            params,
            weight_in,
            bias_in,
            weight_mid,
            bias_mid,
            weight_out,
            bias_out,
            pca_basis,
            offset,
        )
    local_waves = bessel.shape[0]
    total_waves = sources.shape[1]
    cosmos = params.shape[1]
    first_wave = lax.axis_index("ka") * local_waves
    factor = primordial(params, window_low, window_high, first_wave, local_waves, total_waves)
    regrouped = lax.all_to_all(sources, "ka", split_axis=1, concat_axis=0, tiled=True)
    transfer = jnp.einsum("tkc,ktl->klc", regrouped, bessel, preferred_element_type=jnp.float32)
    power = lax.psum_scatter(
        jnp.einsum("klc,kc->lc", transfer * transfer, factor, precision=lax.Precision.HIGHEST),
        "ka",
        scatter_dimension=0,
        tiled=True,
    )
    degree = multipoles.astype(jnp.float32)
    smoothing = jnp.exp(-2.0 * degree * (degree + 1.0) / (LMAX * (LMAX + 1.0)))
    spectra = smoothing[:, None] * power
    inner_pre = mat(weight_in, params) + bias_in[:, None]
    inner_act = jax.nn.silu(inner_pre)
    middle_pre = mat(weight_mid, inner_act) + bias_mid[:, None]
    middle_act = jax.nn.silu(middle_pre)
    coeffs = mat(weight_out, middle_act) + bias_out[:, None]
    residual = offset[:, None] + mat(pca_basis, coeffs) - spectra
    grad_basis = mat(residual, coeffs.T) / cosmos
    coef_part = mat(pca_basis.T, residual) / cosmos
    coef_grad = lax.psum(coef_part, "ka")
    grad_in, grad_mid, grad_out = backward(
        coef_grad, inner_pre, inner_act, middle_pre, middle_act, params, weight_mid, weight_out
    )
    return (spectra, grad_basis, grad_in, grad_mid, grad_out)


def lands(n, sources, bessel, basis):
    times, _, cosmos = sources.shape
    levels = n // FAN
    return (
        2 * times == LANES
        and FAN * bessel.shape[0] == LANES
        and cosmos == 32
        and n % FAN == 0
        and levels in (2, 4)
        and basis.shape == (32, 64)
        and bessel.shape[2] % LANES == 0
        and bessel.size * 2 <= 32 * 1024 * 1024
    )


def solution(mesh):
    return jax.shard_map(
        functools.partial(local, mesh.shape["ka"]),
        mesh=mesh,
        in_specs=(
            P("ka", None, "grp"),
            P("ka", None, None),
            P("ka"),
            P("grp"),
            P("grp"),
            P(None, "grp"),
            P(),
            P(),
            P(),
            P(),
            P(),
            P(),
            P("ka", None),
            P("ka"),
        ),
        out_specs=(
            P("ka", "grp"),
            P(("grp", "ka"), None),
            P("grp", None),
            P("grp", None),
            P("grp", None),
        ),
        check_vma=False,
    )
```

```python
import functools
import math

import jax
import jax.numpy as jnp
from jax import lax
from jax.experimental import pallas as pl
from jax.experimental.pallas import tpu as pltpu
from jax.sharding import PartitionSpec as P

MESH = pl.DeviceIdType.MESH
LANES = 128
FAN = 4
SMALL = 12

LMAX = 5000


def primordial(params, window_low, window_high, first_wave, wave_count, total_waves):
    wave_index = first_wave + jnp.arange(wave_count, dtype=jnp.int32)
    log_ratio = math.log(0.002) + wave_index.astype(jnp.float32) * (math.log(5000.0) / total_waves)
    tilted = 0.5 * params[0][None, :] + 0.3 * params[1][None, :] * log_ratio[:, None]
    inside = (wave_index[:, None] >= window_low[None, :]) & (
        wave_index[:, None] < window_high[None, :]
    )
    return jnp.where(inside, jnp.exp(tilted), jnp.zeros_like(tilted)) / total_waves


def silu_slope(value):
    sigma = jax.nn.sigmoid(value)
    return sigma * (1.0 + value * (1.0 - sigma))


def mat(left, right):
    return jnp.dot(left, right, precision=lax.Precision.HIGHEST)


def backward(
    coef_grad, inner_pre, inner_act, middle_pre, middle_act, params, weight_mid, weight_out
):
    grad_out = mat(coef_grad, middle_act.T)
    middle_delta = mat(weight_out.T, coef_grad) * silu_slope(middle_pre)
    grad_mid = mat(middle_delta, inner_act.T)
    inner_delta = mat(weight_mid.T, middle_delta) * silu_slope(inner_pre)
    grad_in = mat(inner_delta, params.T)
    return (grad_in, grad_mid, grad_out)


def contract(left, right, left_dim, right_dim):
    return lax.dot_general(
        left,
        right,
        (((left_dim,), (right_dim,)), ((), ())),
        precision=lax.Precision.HIGHEST,
        preferred_element_type=jnp.float32,
    )


def by_group(rows_of, groups, rows):
    lane_group = lax.broadcasted_iota(jnp.int32, (rows, LANES), 1) // (LANES // groups)
    packed = rows_of(0)
    for g in range(1, groups):
        packed = jnp.where(lane_group == g, rows_of(g), packed)
    return packed


def unpacked(packed, groups):
    lane_group = lax.broadcasted_iota(jnp.int32, packed.shape, 1) // (LANES // groups)
    return jnp.concatenate([jnp.where(lane_group == g, packed, 0.0) for g in range(groups)], axis=0)


def flipped(level, bits, levels):
    result, weight = 0, 1
    while weight < levels:
        bit = lax.rem(level // weight, 2)
        result = result + weight * (1 - bit if bits // weight % 2 else bit)
        weight *= 2
    return result


def transfer_kernel(n, source_hbm, bessel_ref, *refs):
    small_hbm, outs, small, scratch = refs[:SMALL], refs[SMALL : SMALL + 6], refs[SMALL + 6 : 2 * SMALL + 6], refs[2 * SMALL + 6 :]
    multipoles_ref, low_ref, high_ref, params_ref, weight_in_ref, bias_in_ref = small[:6]
    weight_mid_ref, bias_mid_ref, weight_out_ref, bias_out_ref, basis_ref, offset_ref = small[6:]
    inner_ref, middle_ref, coeffs_ref, spectra_ref, residual_ref, coef_ref = outs
    source_ref, source_sem, small_sem, part_ref, power_out, power_in, coef_out, coef_in = scratch[:8]
    send_power, recv_power, send_coef, recv_coef, wide, turned, packed, landed, kernels, total = scratch[8:18]
    send_sem, recv_sem, load_sem = scratch[18:]
    times, cosmos, total_waves = source_hbm.shape
    waves = bessel_ref.shape[0]
    half = cosmos // 2
    levels = n // FAN
    me = lax.axis_index("ka")
    my_level, my_place = me // FAN, lax.rem(me, FAN)

    barrier = pltpu.get_barrier_semaphore()
    for step in range(1, n):
        peer = lax.rem(me + step, n)
        pl.semaphore_signal(barrier, inc=1, device_id={"ka": peer}, device_id_type=MESH)

    far_first = sorted(range(1, levels), key=lambda i: (-(i // (levels // 2)), i)) + [0]
    fetches = {}
    for i in far_first:
        lanes = pl.ds(pl.multiple_of(flipped(my_level, i, levels) * LANES, LANES), LANES)
        fetches[i] = pltpu.make_async_copy(source_hbm.at[:, :, lanes], source_ref.at[i], source_sem.at[i])
        fetches[i].start()
    small_loads = []
    for index in range(SMALL):
        load = pltpu.make_async_copy(small_hbm[index], small[index], small_sem.at[index])
        load.start()
        small_loads.append(load)
    loads = []
    for i in range(levels):
        span = pl.ds(pl.multiple_of(flipped(my_level, i, levels) * (FAN * times), FAN * times), FAN * times)
        load = pltpu.make_async_copy(bessel_ref.at[:, span, :], kernels.at[i], load_sem.at[i])
        load.start()
        loads.append(load)

    copies = {}
    for position, i in enumerate(far_first):
        level = flipped(my_level, i, levels)
        fetches[i].wait()
        wide[...] = source_ref[i].astype(jnp.float32).reshape(times * cosmos, LANES)
        for c in range(half):
            pair = jnp.concatenate(
                [wide[pl.ds(c, times, stride=cosmos), :], wide[pl.ds(c + half, times, stride=cosmos), :]], axis=0
            )
            turned[pl.ds(c, LANES, stride=half), :] = pair.T
        packed[pl.ds(level * FAN, FAN)] = turned[...].astype(jnp.bfloat16).reshape(FAN, waves * half, LANES)
        if position == 0:
            pl.semaphore_wait(barrier, n - 1)
        for step in range(FAN):
            if i == 0 and step == 0:
                continue
            peer = level * FAN + lax.rem(my_place + step, FAN)
            copy = pltpu.make_async_remote_copy(
                src_ref=packed.at[peer],
                dst_ref=landed.at[me],
                send_sem=send_sem.at[i * FAN + step],
                recv_sem=recv_sem.at[i * FAN + step],
                device_id={"ka": peer},
                device_id_type=MESH,
            )
            copy.start()
            copies[i, step] = copy
    landed[me] = packed[me]
    part_ref[...] = jnp.zeros_like(part_ref)

    for load in small_loads:
        load.wait()
    params = params_ref[...]
    groups, rows = LANES // basis_ref.shape[0], cosmos * basis_ref.shape[0] // LANES
    inner = contract(params, weight_in_ref[...], 0, 0) + bias_in_ref[...]
    inner_ref[...] = inner
    middle = contract(jax.nn.silu(inner), weight_mid_ref[...], 1, 1) + bias_mid_ref[...]
    middle_ref[...] = middle
    coeffs = contract(jax.nn.silu(middle), weight_out_ref[...], 1, 1) + bias_out_ref[...]
    coeffs_ref[...] = coeffs
    basis = jnp.concatenate([basis_ref[...]] * groups, axis=0)
    own = basis_ref.shape[0]
    spread = (
        lax.broadcasted_iota(jnp.int32, (own, LANES), 0) == lax.broadcasted_iota(jnp.int32, (own, LANES), 1) % own
    ).astype(jnp.float32)
    base = contract(coeffs, basis, 1, 1) + contract(offset_ref[...], spread, 1, 0)
    base = by_group(lambda g: base[g * rows : (g + 1) * rows], groups, rows)
    degree = contract(multipoles_ref[...].astype(jnp.float32), spread, 1, 0)
    smoothing = jnp.exp(-2.0 * degree * (degree + 1.0) / (LMAX * (LMAX + 1.0)))

    def column(row):
        return contract(row, jnp.ones((1, LANES), jnp.float32), 0, 0)

    amplitude, tilt = column(params_ref[0:1, :]), column(params_ref[1:2, :])
    low, high = column(low_ref[...].astype(jnp.float32)), column(high_ref[...].astype(jnp.float32))

    def factor(k):
        index = (me * waves + k).astype(jnp.float32)
        log_ratio = math.log(0.002) + index * (math.log(5000.0) / total_waves)
        tilted = 0.5 * amplitude + 0.3 * tilt * log_ratio
        inside = (index >= low) & (index < high)
        value = jnp.where(inside, jnp.exp(tilted), 0.0) / total_waves
        return jnp.concatenate([value] * (part_ref.shape[1] // LANES), axis=1)

    low_lanes = lax.broadcasted_iota(jnp.int32, (half, LANES), 1) < times

    def joined(first, second):
        first, second = first.astype(jnp.float32), second.astype(jnp.float32)
        low = jnp.where(low_lanes, first, pltpu.roll(second, times, 1))
        high = jnp.where(low_lanes, pltpu.roll(first, times, 1), second)
        return jnp.concatenate([low, high], axis=0).astype(jnp.bfloat16)

    for i in range(levels):
        level = flipped(my_level, i, levels)
        for step in range(FAN):
            if (i, step) in copies:
                copies[i, step].wait_recv()
        loads[i].wait()

        def wave(k, carry, i=i, level=level):
            rows = pl.ds(pl.multiple_of(k * half, half), half)
            blocks = [landed[level * FAN + place, rows, :] for place in range(FAN)]
            left = jnp.concatenate([joined(*blocks[p : p + 2]) for p in range(0, FAN, 2)], axis=1)
            product = jnp.dot(left, kernels[i, k], preferred_element_type=jnp.float32)
            if i > 0:
                product = product + total[k]
            if i < levels - 1:
                total[k] = product
            else:
                part_ref[...] += factor(k) * product * product
            return carry

        lax.fori_loop(0, waves, wave, 0, unroll=4)
    for copy in copies.values():
        copy.wait_send()

    def scatter(source_of, landing, send, recv):
        started = []
        for step in range(1, n):
            peer = lax.rem(me + step, n)
            copy = pltpu.make_async_remote_copy(
                src_ref=source_of(peer),
                dst_ref=landing.at[me],
                send_sem=send.at[step],
                recv_sem=recv.at[step],
                device_id={"ka": peer},
                device_id_type=MESH,
            )
            copy.start()
            started.append(copy)
        return started

    for peer in range(n):
        lane, shift = peer * own // LANES * LANES, peer * own % LANES
        power_out[peer] = by_group(
            lambda g: pltpu.roll(
                part_ref[g * rows : (g + 1) * rows, lane : lane + LANES], (g * own - shift) % LANES, 1
            ),
            groups,
            rows,
        )
    started = scatter(lambda peer: power_out.at[peer], power_in, send_power, recv_power)
    power_in[me] = power_out[me]
    for copy in started:
        copy.wait()
    spectra = smoothing * jnp.sum(power_in[...], axis=0)
    spectra_ref[...] = spectra
    residual = base - spectra
    residual_ref[...] = residual
    gradient = contract(unpacked(residual, groups), jnp.concatenate([basis, basis], axis=1), 1, 0) / cosmos
    coef_out[...] = by_group(lambda g: gradient[g * half : (g + 1) * half], 2, half)
    started = scatter(lambda peer: coef_out, coef_in, send_coef, recv_coef)
    coef_in[me] = coef_out[...]
    for copy in started:
        copy.wait()
    coef_ref[...] = jnp.sum(coef_in[...], axis=0)


def output_kernel(
    inner_ref,
    middle_ref,
    coeffs_ref,
    packed_spectra_ref,
    residual_ref,
    coef_ref,
    params_ref,
    weight_mid_ref,
    weight_out_ref,
    spectra_ref,
    grad_basis_ref,
    grad_in_ref,
    grad_mid_ref,
    grad_out_ref,
):
    own, components = grad_basis_ref.shape
    groups = LANES // own
    cosmos = params_ref.shape[1]

    def folded(rows):
        total = rows[:own]
        for g in range(1, groups):
            total = total + rows[g * own : (g + 1) * own]
        return total

    spectra_ref[...] = folded(unpacked(packed_spectra_ref[...], groups).T)
    grad_basis_ref[...] = folded(contract(unpacked(residual_ref[...], groups), coeffs_ref[...], 0, 0)) / cosmos
    coef = coef_ref[...]
    coef = jnp.concatenate([coef, pltpu.roll(coef, components, 1)], axis=0)[:, :components]
    inner, middle = inner_ref[...], middle_ref[...]
    grad_out_ref[...] = contract(coef, jax.nn.silu(middle), 0, 0)
    middle_delta = contract(coef, weight_out_ref[...], 1, 0) * silu_slope(middle)
    grad_mid_ref[...] = contract(middle_delta, jax.nn.silu(inner), 0, 0)
    inner_delta = contract(middle_delta, weight_mid_ref[...], 1, 0) * silu_slope(inner)
    grad_in_ref[...] = contract(params_ref[...], inner_delta, 1, 0)


def landed(
    n,
    sources,
    bessel,
    multipoles,
    window_low,
    window_high,
    params,
    weight_in,
    bias_in,
    weight_mid,
    bias_mid,
    weight_out,
    bias_out,
    pca_basis,
    offset,
):
    times, _, cosmos = sources.shape
    waves, _, all_multipoles = bessel.shape
    hidden, (own, components) = weight_mid.shape[0], pca_basis.shape
    levels = n // FAN
    block = (n, waves * cosmos // 2, LANES)
    power_block, coef_block = (cosmos * own // LANES, LANES), (cosmos // 2, LANES)
    vmem = pl.BlockSpec(memory_space=pltpu.VMEM)
    small = (
        multipoles[None, :],
        window_low[None, :],
        window_high[None, :],
        params,
        weight_in.T,
        bias_in[None, :],
        weight_mid,
        bias_mid[None, :],
        weight_out,
        bias_out[None, :],
        pca_basis,
        offset[None, :],
    )
    results = pl.pallas_call(
        functools.partial(transfer_kernel, n),
        out_shape=[
            jax.ShapeDtypeStruct(shape, jnp.float32)
            for shape in (
                (cosmos, hidden),
                (cosmos, hidden),
                (cosmos, components),
                power_block,
                power_block,
                coef_block,
            )
        ],
        in_specs=[pl.BlockSpec(memory_space=pl.ANY)] * (2 + SMALL),
        out_specs=[vmem] * 6,
        scratch_shapes=[pltpu.VMEM(array.shape, array.dtype) for array in small]
        + [
            pltpu.VMEM((levels, times, cosmos, LANES), jnp.bfloat16),
            pltpu.SemaphoreType.DMA((levels,)),
            pltpu.SemaphoreType.DMA((SMALL,)),
            pltpu.VMEM((cosmos, all_multipoles), jnp.float32),
            pltpu.VMEM((n,) + power_block, jnp.float32),
            pltpu.VMEM((n,) + power_block, jnp.float32),
            pltpu.VMEM(coef_block, jnp.float32),
            pltpu.VMEM((n,) + coef_block, jnp.float32),
        ]
        + [pltpu.SemaphoreType.DMA((n,))] * 4
        + [
            pltpu.VMEM((times * cosmos, LANES), jnp.float32),
            pltpu.VMEM((LANES * cosmos // 2, LANES), jnp.float32),
            pltpu.VMEM(block, jnp.bfloat16),
            pltpu.VMEM(block, jnp.bfloat16),
            pltpu.VMEM((levels, waves, FAN * times, all_multipoles), jnp.bfloat16),
            pltpu.VMEM((waves, cosmos, all_multipoles), jnp.float32),
            pltpu.SemaphoreType.DMA((n,)),
            pltpu.SemaphoreType.DMA((n,)),
            pltpu.SemaphoreType.DMA((levels,)),
        ],
        compiler_params=pltpu.CompilerParams(
            collective_id=0, has_side_effects=True, vmem_limit_bytes=62 * 1024 * 1024
        ),
    )(
        sources.transpose(0, 2, 1),
        bessel,
        *small,
    )
    spectra, grad_basis, grad_in, grad_mid, grad_out = pl.pallas_call(
        output_kernel,
        out_shape=[
            jax.ShapeDtypeStruct(shape, jnp.float32)
            for shape in (
                (own, cosmos),
                (own, components),
                (params.shape[0], hidden),
                (hidden, hidden),
                (components, hidden),
            )
        ],
        in_specs=[vmem] * 9,
        out_specs=[vmem] * 5,
    )(*results, params, weight_mid, weight_out)
    return (spectra, grad_basis, grad_in.T, grad_mid, grad_out)


def local(
    n,
    sources,
    bessel,
    multipoles,
    window_low,
    window_high,
    params,
    weight_in,
    bias_in,
    weight_mid,
    bias_mid,
    weight_out,
    bias_out,
    pca_basis,
    offset,
):
    if lands(n, sources, bessel, pca_basis):
        return landed(
            n,
            sources,
            bessel,
            multipoles,
            window_low,
            window_high,
            params,
            weight_in,
            bias_in,
            weight_mid,
            bias_mid,
            weight_out,
            bias_out,
            pca_basis,
            offset,
        )
    local_waves = bessel.shape[0]
    total_waves = sources.shape[1]
    cosmos = params.shape[1]
    first_wave = lax.axis_index("ka") * local_waves
    factor = primordial(params, window_low, window_high, first_wave, local_waves, total_waves)
    regrouped = lax.all_to_all(sources, "ka", split_axis=1, concat_axis=0, tiled=True)
    transfer = jnp.einsum("tkc,ktl->klc", regrouped, bessel, preferred_element_type=jnp.float32)
    power = lax.psum_scatter(
        jnp.einsum("klc,kc->lc", transfer * transfer, factor, precision=lax.Precision.HIGHEST),
        "ka",
        scatter_dimension=0,
        tiled=True,
    )
    degree = multipoles.astype(jnp.float32)
    smoothing = jnp.exp(-2.0 * degree * (degree + 1.0) / (LMAX * (LMAX + 1.0)))
    spectra = smoothing[:, None] * power
    inner_pre = mat(weight_in, params) + bias_in[:, None]
    inner_act = jax.nn.silu(inner_pre)
    middle_pre = mat(weight_mid, inner_act) + bias_mid[:, None]
    middle_act = jax.nn.silu(middle_pre)
    coeffs = mat(weight_out, middle_act) + bias_out[:, None]
    residual = offset[:, None] + mat(pca_basis, coeffs) - spectra
    grad_basis = mat(residual, coeffs.T) / cosmos
    coef_part = mat(pca_basis.T, residual) / cosmos
    coef_grad = lax.psum(coef_part, "ka")
    grad_in, grad_mid, grad_out = backward(
        coef_grad, inner_pre, inner_act, middle_pre, middle_act, params, weight_mid, weight_out
    )
    return (spectra, grad_basis, grad_in, grad_mid, grad_out)


def lands(n, sources, bessel, basis):
    times, _, cosmos = sources.shape
    levels = n // FAN
    return (
        2 * times == LANES
        and FAN * bessel.shape[0] == LANES
        and cosmos == 32
        and n % FAN == 0
        and levels in (2, 4)
        and basis.shape == (32, 64)
        and bessel.shape[2] % LANES == 0
        and bessel.size * 2 <= 32 * 1024 * 1024
    )


def solution(mesh):
    return jax.shard_map(
        functools.partial(local, mesh.shape["ka"]),
        mesh=mesh,
        in_specs=(
            P("ka", None, "grp"),
            P("ka", None, None),
            P("ka"),
            P("grp"),
            P("grp"),
            P(None, "grp"),
            P(),
            P(),
            P(),
            P(),
            P(),
            P(),
            P("ka", None),
            P("ka"),
        ),
        out_specs=(
            P("ka", "grp"),
            P(("grp", "ka"), None),
            P("grp", None),
            P("grp", None),
            P("grp", None),
        ),
        check_vma=False,
    )
```
